32 devices in a mesh: slab: 8 (over z, y), col: 4 (over x, core).
Axes of the slice: x: 2, y: 2, z: 4, core: 2. Of those that a mesh axis runs over, the one named last changes fastest.
Arguments:
- classes: int32 [64, 512], P(('slab', 'col')), may hold values from 0 to 15
- across_coeff: float32 [16], replicated, may hold values from 0.5 to 5
- along_coeff: float32 [16], replicated, may hold values from 0.05 to 0.5
Outputs:
- piece_maps: float32 [32768, 1024], P(('slab', 'col'))
- root_map: float32 [1024, 1024], P(('slab', 'col'))
The draws below stay inside these ranges and needn't reach their ends.
All inputs are finite; a program needn't handle non-finite values.
Results may differ from the reference program's by a relative error of at most 0.0003.
Values sent between devices are 32-bit elements; how exact they have to be, the bound alone decides.
A program may use at most 128 MiB of HBM per device.

```python
import math
from functools import partial
import jax
import jax.numpy as jnp
from jax import lax

E = 512
C = 2
CLASSES = 16
PIECES = 32
COLS = 64


def plant(array, rng, low, high):
    spot = [jax.random.randint(jax.random.fold_in(rng, axis), (), 0, length) for axis, length in enumerate(array.shape)]
    widest = array.shape.index(max(array.shape))
    neighbour = spot[:widest] + [(spot[widest] + 1) % array.shape[widest]] + spot[widest + 1:]
    return array.at[tuple(spot)].set(low).at[tuple(neighbour)].set(high)


def setup_inputs(seed: int = 0) -> dict:
    key_of = jax.random.split(jax.random.key(seed), 4)
    classes = plant(jax.random.randint(key_of[0], (COLS, E), 0, CLASSES), jax.random.fold_in(key_of[0], 1), 0, CLASSES - 1).astype(jnp.int32)
    across_coeff = jnp.clip(jnp.exp(jax.random.uniform(key_of[1], (CLASSES,), jnp.float32, math.log(0.5), math.log(5.0))), 0.5, 5.0)
    along_coeff = jnp.clip(jnp.exp(jax.random.uniform(key_of[2], (CLASSES,), jnp.float32, math.log(0.05), math.log(0.5))), 0.05, 0.5)
    return {"classes": classes, "across_coeff": across_coeff, "along_coeff": along_coeff}


def lookup(classes, values_table):
    levels = jnp.arange(values_table.shape[0], dtype=jnp.int32)
    matches = classes[:, None, :] == levels[None, :, None]
    return jnp.sum(jnp.where(matches, values_table[None, :, None], 0.0), axis=1)

def strip_map(along_col, across_col):
    half_size = along_col.shape[0]
    row_index = lax.broadcasted_iota(jnp.int32, (half_size, half_size), 0)
    col_index = lax.broadcasted_iota(jnp.int32, (half_size, half_size), 1)
    shifted = jnp.roll(along_col, 1)
    vertical = jnp.where(row_index == col_index, (along_col + shifted)[None, :], 0.0)
    vertical = vertical - jnp.where(col_index == (row_index + 1) % half_size, along_col[:, None], 0.0)
    vertical = vertical - jnp.where(row_index == (col_index + 1) % half_size, along_col[None, :], 0.0)
    across_diag = jnp.where(row_index == col_index, across_col[None, :], 0.0)
    upper_rows = jnp.concatenate([vertical + across_diag, -across_diag], axis=1)
    lower_rows = jnp.concatenate([-across_diag, across_diag], axis=1)
    return jnp.concatenate([upper_rows, lower_rows], axis=0)

def quarters(full_map):
    half_size = full_map.shape[0] // 2
    return (full_map[:half_size, :half_size], full_map[:half_size, half_size:], full_map[half_size:, :half_size], full_map[half_size:, half_size:])

def merge_blocks(left_upper, left_lower_left, left_lower, right_upper, right_upper_right, right_lower):
    half_size = left_upper.shape[0]
    factor = jnp.linalg.cholesky(left_lower + right_upper)
    coupled = jnp.concatenate([left_lower_left, right_upper_right], axis=1)
    scaled = lax.linalg.triangular_solve(factor, coupled, left_side=True, lower=True)
    product = lax.dot_general(scaled, scaled, (((0,), (0,)), ((), ())), precision=lax.Precision.HIGHEST)
    zero_block = jnp.zeros((half_size, half_size), left_upper.dtype)
    diagonal_part = jnp.concatenate([jnp.concatenate([left_upper, zero_block], axis=1), jnp.concatenate([zero_block, right_lower], axis=1)], axis=0)
    return diagonal_part - product

def merge_maps(left_map, right_map):
    left_upper, left_upper_right, left_lower_left, left_lower = quarters(left_map)
    right_upper, right_upper_right, right_lower_left, right_lower = quarters(right_map)
    return merge_blocks(left_upper, left_lower_left, left_lower, right_upper, right_upper_right, right_lower)

def build_piece(piece_classes, across_coeff, along_coeff):
    across = lookup(piece_classes, across_coeff)
    along = lookup(piece_classes, along_coeff)
    own_map = strip_map(along[0], across[0])
    for column in range(1, piece_classes.shape[0]):
        own_map = merge_maps(own_map, strip_map(along[column], across[column]))
    return own_map

def advance(running, own_map):
    return (merge_maps(running, own_map), None)

def reference(classes, across_coeff, along_coeff):
    grouped = classes.reshape(PIECES, C, E)
    pieces = lax.map(partial(build_piece, across_coeff=across_coeff, along_coeff=along_coeff), grouped)
    root_map, unused = lax.scan(advance, pieces[0], pieces[1:])
    return (pieces.reshape(PIECES * 2 * E, 2 * E), root_map)
```

```python
import functools
import jax
import jax.numpy as jnp
from jax import lax
from jax.experimental import pallas as pl
from jax.experimental.pallas import tpu as pltpu
from jax.sharding import PartitionSpec as P

HIGHEST = lax.Precision.HIGHEST
AXES = ("slab", "col")


def swapped(block, axis, stride):
    count = lax.axis_size(axis)
    route = []
    for low in range(count):
        high = low | 1 << stride
        if high != low and high < count:
            route += [(low, high), (high, low)]
    return lax.ppermute(block, axis, route)


def lookup(classes, values_table):
    levels = jnp.arange(values_table.shape[0], dtype=jnp.int32)
    matches = classes[:, None, :] == levels[None, :, None]
    return jnp.sum(jnp.where(matches, values_table[None, :, None], 0.0), axis=1)


def strip_map(along_col, across_col):
    half_size = along_col.shape[0]
    row_index = lax.broadcasted_iota(jnp.int32, (half_size, half_size), 0)
    col_index = lax.broadcasted_iota(jnp.int32, (half_size, half_size), 1)
    shifted = jnp.roll(along_col, 1)
    vertical = jnp.where(row_index == col_index, (along_col + shifted)[None, :], 0.0)
    vertical = vertical - jnp.where(
        col_index == (row_index + 1) % half_size, along_col[:, None], 0.0
    )
    vertical = vertical - jnp.where(
        row_index == (col_index + 1) % half_size, along_col[None, :], 0.0
    )
    across_diag = jnp.where(row_index == col_index, across_col[None, :], 0.0)
    upper_rows = jnp.concatenate([vertical + across_diag, -across_diag], axis=1)
    lower_rows = jnp.concatenate([-across_diag, across_diag], axis=1)
    return jnp.concatenate([upper_rows, lower_rows], axis=0)


def quarters(full_map):
    half_size = full_map.shape[0] // 2
    return (
        full_map[:half_size, :half_size],
        full_map[:half_size, half_size:],
        full_map[half_size:, :half_size],
        full_map[half_size:, half_size:],
    )


def blocked_factor(matrix):
    size_total = matrix.shape[0]
    panel = 128
    columns = []
    remaining = matrix
    for start in range(0, size_total, panel):
        head = remaining[:panel, :panel]
        head_factor = jnp.linalg.cholesky(head)
        if remaining.shape[0] > panel:
            below = remaining[panel:, :panel]
            below_factor = lax.linalg.triangular_solve(
                head_factor, below, left_side=False, lower=True, transpose_a=True
            )
            remaining = remaining[panel:, panel:] - lax.dot_general(
                below_factor,
                below_factor,
                (((1,), (1,)), ((), ())),
                precision=lax.Precision.HIGHEST,
            )
            block_column = jnp.concatenate([head_factor, below_factor], axis=0)
        else:
            block_column = head_factor
        if start > 0:
            block_column = jnp.concatenate(
                [jnp.zeros((start, panel), matrix.dtype), block_column], axis=0
            )
        columns.append(block_column)
    return jnp.concatenate(columns, axis=1)


def merge_blocks(
    left_upper, left_lower_left, left_lower, right_upper, right_upper_right, right_lower
):
    half_size = left_upper.shape[0]
    factor = blocked_factor(left_lower + right_upper)
    coupled = jnp.concatenate([left_lower_left, right_upper_right], axis=1)
    scaled = lax.linalg.triangular_solve(factor, coupled, left_side=True, lower=True)
    product = lax.dot_general(
        scaled, scaled, (((0,), (0,)), ((), ())), precision=lax.Precision.HIGHEST
    )
    zero_block = jnp.zeros((half_size, half_size), left_upper.dtype)
    diagonal_part = jnp.concatenate(
        [
            jnp.concatenate([left_upper, zero_block], axis=1),
            jnp.concatenate([zero_block, right_lower], axis=1),
        ],
        axis=0,
    )
    return diagonal_part - product


def merge_maps(left_map, right_map):
    left_upper, left_upper_right, left_lower_left, left_lower = quarters(left_map)
    right_upper, right_upper_right, right_lower_left, right_lower = quarters(right_map)
    return merge_blocks(
        left_upper, left_lower_left, left_lower, right_upper, right_upper_right, right_lower
    )


def level_payload(merged, is_right):
    upper, upper_right, lower_left, lower = quarters(merged)
    middle = jnp.where(is_right, upper_right, lower_left)
    payload = jnp.stack([upper, middle, lower])
    return payload


def joined(merged, received, is_right):
    upper, upper_right, lower_left, lower = quarters(merged)
    partner_upper = received[0]
    partner_middle = received[1]
    partner_lower = received[2]
    left_upper = jnp.where(is_right, partner_upper, upper)
    left_lower_left = jnp.where(is_right, partner_middle, lower_left)
    left_lower = jnp.where(is_right, partner_lower, lower)
    right_upper = jnp.where(is_right, upper, partner_upper)
    right_upper_right = jnp.where(is_right, upper_right, partner_middle)
    right_lower = jnp.where(is_right, lower, partner_lower)
    return merge_blocks(
        left_upper, left_lower_left, left_lower, right_upper, right_upper_right, right_lower
    )


def local_columns(classes, across_coeff, along_coeff):
    across = lookup(classes, across_coeff)
    along = lookup(classes, along_coeff)
    own_map = piece_map(across, along)
    col_levels = lax.axis_size("col").bit_length() - 1
    slab_levels = lax.axis_size("slab").bit_length() - 1
    merged = own_map
    for height in range(col_levels):
        is_right = lax.axis_index("col") >> height & 1 == 1
        received = swapped(level_payload(merged, is_right), "col", height)
        merged = joined(merged, received, is_right)
    for height in range(slab_levels):
        is_right = lax.axis_index("slab") >> height & 1 == 1
        received = swapped(level_payload(merged, is_right), "slab", height)
        merged = joined(merged, received, is_right)
    share_rows = merged.shape[0] // lax.axis_size(("slab", "col"))
    root_rows = lax.dynamic_slice_in_dim(
        merged, lax.axis_index(("slab", "col")) * share_rows, share_rows, 0
    )
    return (own_map, root_rows)


def sweep_kernel(count, size, x_ref, o_ref):
    o_ref[...] = x_ref[...]
    sub = lax.broadcasted_iota(jnp.int32, (1, size, size), 1)
    lane = lax.broadcasted_iota(jnp.int32, (1, size, size), 2)

    def step(k, carry):
        group = min(count, 4)
        for start in range(0, count, group):
            a = o_ref[start : start + group]
            row = o_ref[start : start + group, pl.ds(k, 1), :]
            is_row = sub == k
            is_col = lane == k
            col = jnp.sum(jnp.where(is_col, a, 0.0), axis=2, keepdims=True)
            pivot = jnp.sum(jnp.where(is_col[:, :1], row, 0.0), axis=2, keepdims=True)
            inv = 1.0 / pivot
            scaled = row * inv
            new = a - col * scaled
            new = jnp.where(is_col, -(col * inv), new)
            new = jnp.where(is_row, jnp.where(is_col, inv, scaled), new)
            o_ref[start : start + group] = new
        return carry

    lax.fori_loop(0, size, step, 0)


def inverses(blocks):
    count, size, _ = blocks.shape
    return pl.pallas_call(
        functools.partial(sweep_kernel, count, size),
        out_shape=jax.ShapeDtypeStruct(blocks.shape, jnp.float32),
        in_specs=[pl.BlockSpec(memory_space=pltpu.VMEM)],
        out_specs=pl.BlockSpec(memory_space=pltpu.VMEM),
    )(blocks)


def piece_kernel(size, rows, vec_ref, cols_ref, o_ref, coef):
    levels = size.bit_length() - 1
    i = pl.program_id(0)

    def back(x, s):
        return pltpu.roll(x, s, 1)

    def fore(x, s):
        return pltpu.roll(x, size - s, 1)

    @pl.when(i == 0)
    def _():
        def wide(k):
            return jnp.broadcast_to(vec_ref[k : k + 1, :], (8, size))

        a0, a1, al0, al1 = wide(0), wide(1), wide(2), wide(3)
        sh1 = back(al1, 1)
        diag = a0 + a1 + al1 + sh1
        inv = 1.0 / diag
        coef[0] = inv
        lo = -sh1 * inv
        hi = -al1 * inv
        for level in range(levels - 1):
            s = 1 << level
            fix = 1.0 / (1.0 - lo * back(hi, s) - hi * fore(lo, s))
            coef[3 * level + 1] = -lo
            coef[3 * level + 2] = -hi
            coef[3 * level + 3] = fix
            lo, hi = -lo * back(lo, s) * fix, -hi * fore(hi, s) * fix
        g = lo + hi
        h = back(g, size // 2)
        coef[3 * levels - 2] = -g
        coef[3 * levels - 1] = 1.0 / (1.0 - g * h)

    def co(k):
        return coef[k, 0:1, :]

    row = lax.broadcasted_iota(jnp.int32, (rows, size), 0) + i * rows
    col = lax.broadcasted_iota(jnp.int32, (rows, size), 1)
    x = jnp.where(row == col, co(0), 0.0)
    for level in range(levels - 1):
        s = 1 << level
        x = (x + co(3 * level + 1) * back(x, s) + co(3 * level + 2) * fore(x, s)) * co(3 * level + 3)
    x = (x + co(3 * levels - 2) * back(x, size // 2)) * co(3 * levels - 1)
    a0, a1, al0 = vec_ref[0:1, :], vec_ref[1:2, :], vec_ref[2:3, :]
    sh0 = jnp.broadcast_to(vec_ref[4:5, :], (1, size))
    r0, r1 = cols_ref[:, 0:1], cols_ref[:, 1:2]
    vert = jnp.where(row == col, al0 + sh0 + a0, 0.0)
    vert = vert - jnp.where(row == jnp.where(col == size - 1, 0, col + 1), al0, 0.0)
    vert = vert - jnp.where(col == jnp.where(row == size - 1, 0, row + 1), sh0, 0.0)
    x0, x1 = x * a0, x * a1
    o_ref[0, :, :size] = vert - r0 * x0
    o_ref[0, :, size:] = -(r0 * x1)
    o_ref[1, :, :size] = -(r1 * x0)
    o_ref[1, :, size:] = jnp.where(row == col, a1, 0.0) - r1 * x1


def piece_map(across, along):
    size = across.shape[1]
    rows = 32
    vecs = jnp.concatenate([across, along, jnp.roll(along, 1, axis=1), along], axis=0)
    out = pl.pallas_call(
        functools.partial(piece_kernel, size, rows),
        grid=(size // rows,),
        out_shape=jax.ShapeDtypeStruct((2, size, 2 * size), jnp.float32),
        in_specs=[
            pl.BlockSpec((8, size), lambda i: (0, 0)),
            pl.BlockSpec((rows, 2), lambda i: (i, 0)),
        ],
        out_specs=pl.BlockSpec((2, rows, 2 * size), lambda i: (0, i, 0)),
        scratch_shapes=[pltpu.VMEM((3 * (size.bit_length() - 1), 8, size), jnp.float32)],
    )(vecs, across.T)
    return out.reshape(2 * size, 2 * size)


def bmm(a, b):
    return jnp.einsum("bij,bjk->bik", a, b, precision=HIGHEST)


def bmm_t(a, b):
    return jnp.einsum("bji,bjk->bik", a, b, precision=HIGHEST)


def t(a):
    return jnp.swapaxes(a, 1, 2)


def row_elements(across, along_prev, along):
    rows, cols = across.shape
    spot = lax.broadcasted_iota(jnp.int32, (rows, cols), 1)
    inner = spot > 0
    diag = jnp.where(inner, jnp.roll(across, 1, axis=1) + across + along_prev + along, 1.0)
    off = jnp.where(inner, across, 0.0)
    i = lax.broadcasted_iota(jnp.int32, (1, cols, cols), 1)
    j = lax.broadcasted_iota(jnp.int32, (1, cols, cols), 2)
    bb = jnp.where(i == j, diag[:, :, None], 0.0)
    bb = bb - jnp.where(j == i + 1, off[:, :, None], 0.0) - jnp.where(i == j + 1, off[:, None, :], 0.0)
    tb = jnp.where(i == j, -jnp.where(inner, along_prev, 0.0)[:, :, None], 0.0)
    tt = jnp.zeros_like(bb)
    first = jnp.where(spot == 1, -across[:, :1], 0.0)
    last = jnp.where(spot == cols - 1, -across[:, cols - 1 :], 0.0)
    fb = jnp.stack([first, last], axis=2)
    return tt, tb, bb, jnp.zeros_like(fb), fb, jnp.zeros((rows, 2, 2), jnp.float32)


def merge_elements(parts):
    (tta, ttb), (tba, tbb), (bba, bbb), (fta, ftb), (fba, fbb), (kka, kkb) = [
        (p[0::2], p[1::2]) for p in parts
    ]
    n, k = tta.shape[1], fta.shape[2]
    w = jnp.concatenate([t(tba), tbb, fba, ftb], axis=2)
    z = bmm(inverses(bba + ttb), w)
    u = bmm_t(w, z)
    zero = jnp.zeros_like(fta)
    zk = jnp.zeros_like(kka)
    kk = jnp.concatenate(
        [jnp.concatenate([kka, zk], axis=2), jnp.concatenate([zk, kkb], axis=2)], axis=1
    )
    return (
        tta - u[:, :n, :n],
        -u[:, :n, n : 2 * n],
        bbb - u[:, n : 2 * n, n : 2 * n],
        jnp.concatenate([fta, zero], axis=2) - u[:, :n, 2 * n :],
        jnp.concatenate([zero, fbb], axis=2) - u[:, n : 2 * n, 2 * n :],
        kk - u[:, 2 * n :, 2 * n :],
    )


def ring_solve(d, link, rhs):
    count, n = d.shape[0], d.shape[1]
    if count == 1:
        return bmm(inverses(d + link + t(link)), rhs)
    w = jnp.concatenate([t(link[0::2]), link[1::2], rhs[0::2]], axis=2)
    z = bmm(inverses(d[0::2]), w)
    u = bmm_t(w[:, :, : 2 * n], z)
    after = jnp.roll(u, -1, axis=0)
    d_next = d[1::2] - u[:, n:, n : 2 * n] - after[:, :n, :n]
    r_next = rhs[1::2] - u[:, n:, 2 * n :] - after[:, :n, 2 * n :]
    odd = ring_solve(d_next, -u[:, :n, n : 2 * n], r_next)
    both = jnp.concatenate([jnp.roll(odd, 1, axis=0), odd], axis=1)
    even = z[:, :, 2 * n :] - bmm(z[:, :, : 2 * n], both)
    return jnp.stack([even, odd], axis=1).reshape(rhs.shape)


def local_rows(classes, across_coeff, along_coeff):
    own_across = lookup(classes, across_coeff)
    own_along = lookup(classes, along_coeff)
    devices = lax.axis_size(AXES)
    me = lax.axis_index(AXES)
    size = classes.shape[1]
    cols = classes.shape[0] * devices
    height = size // devices
    everyone = lax.all_gather(classes, AXES, axis=0, tiled=True)
    own_map = piece_map(own_across, own_along)
    padded = jnp.concatenate([everyone[:, size - 1 :], everyone], axis=1)
    mine = lax.dynamic_slice_in_dim(padded, me * height, height + 1, 1)
    across = lookup(mine, across_coeff).T
    along = lookup(mine, along_coeff).T
    parts = row_elements(across[1:], along[:-1], along[1:])
    while parts[0].shape[0] > 1:
        parts = merge_elements(parts)
    tt, tb, bb, ft, fb, kk = [p[0] for p in parts]

    def sides(f):
        return f.reshape(f.shape[0], height, 2).swapaxes(1, 2).reshape(f.shape[0], 2 * height)

    ft, fb = sides(ft), sides(fb)
    kk = sides(sides(kk).T)
    square = jnp.concatenate([tt, tb, bb], axis=0)
    square, ft, fb, kk = [
        lax.all_gather(p, AXES, axis=0) for p in (square, ft, fb, kk)
    ]
    tt, tb, bb = square[:, :cols], square[:, cols : 2 * cols], square[:, 2 * cols :]
    share = 2 * size // devices
    start = me * share
    side = start // size
    r0 = start - side * size
    s0 = r0 // height
    strip = lax.broadcasted_iota(jnp.int32, (devices, 1, 1), 0)

    def cut(f, a):
        return lax.dynamic_slice(f, (s0 + a, 0, side * height), (1, f.shape[1], height))[0]

    def at(f, a):
        return jnp.where(strip == s0 + a, f[None], 0.0)

    def rhs_of(f):
        return jnp.concatenate([at(cut(f, 0), 0), at(cut(f, 1), 1)], axis=2)

    rhs = rhs_of(fb) + jnp.roll(rhs_of(ft), -1, axis=0)
    x = ring_solve(bb + jnp.roll(tt, -1, axis=0), tb, rhs)
    x = jnp.concatenate([jnp.roll(x, 1, axis=0), x], axis=1)
    f = jnp.concatenate([ft, fb], axis=1)
    k_rows = jnp.concatenate([at(cut(kk, 0).T, 0), at(cut(kk, 1).T, 1)], axis=1)
    rows = k_rows - bmm_t(x, f)
    rows = rows.reshape(devices, share, 2, height).transpose(1, 2, 0, 3).reshape(share, 2 * size)

    first_ac = lookup(everyone[:1], across_coeff)
    last_ac = lookup(everyone[cols - 1 :], across_coeff)
    al = lookup(everyone[:1], along_coeff)
    sh = jnp.roll(al, 1, axis=1)
    zero = jnp.zeros_like(al)
    on = jnp.concatenate([first_ac + al + sh, last_ac], axis=1)
    below = jnp.concatenate([al, zero], axis=1)
    above = jnp.concatenate([sh, zero], axis=1)
    row = lax.broadcasted_iota(jnp.int32, (share, 2 * size), 0) + start
    col = lax.broadcasted_iota(jnp.int32, (share, 2 * size), 1)
    rows = rows + jnp.where(row == col, on, 0.0)
    rows = rows - jnp.where((row == (col + 1) % size) & (row < size) & (col < size), below, 0.0)
    rows = rows - jnp.where((col == (row + 1) % size) & (row < size) & (col < size), above, 0.0)
    return own_map, rows


def local(classes, across_coeff, along_coeff):
    devices = lax.axis_size(AXES)
    cols = classes.shape[0] * devices
    if 4 * cols <= classes.shape[1]:
        return local_rows(classes, across_coeff, along_coeff)
    return local_columns(classes, across_coeff, along_coeff)


def solution(mesh):
    placed = (P(("slab", "col"), None), P(), P())
    return jax.shard_map(
        local,
        mesh=mesh,
        in_specs=placed,
        out_specs=(P(("slab", "col"), None), P(("slab", "col"), None)),
        check_vma=False,
    )
```

```python
import functools
import jax
import jax.numpy as jnp
from jax import lax
from jax.experimental import pallas as pl
from jax.experimental.pallas import tpu as pltpu
from jax.sharding import PartitionSpec as P

HIGHEST = lax.Precision.HIGHEST
AXES = ("slab", "col")


def swapped(block, axis, stride):
    count = lax.axis_size(axis)
    route = []
    for low in range(count):
        high = low | 1 << stride
        if high != low and high < count:
            route += [(low, high), (high, low)]
    return lax.ppermute(block, axis, route)


def lookup(classes, values_table):
    levels = jnp.arange(values_table.shape[0], dtype=jnp.int32)
    matches = classes[:, None, :] == levels[None, :, None]
    return jnp.sum(jnp.where(matches, values_table[None, :, None], 0.0), axis=1)


def strip_map(along_col, across_col):
    half_size = along_col.shape[0]
    row_index = lax.broadcasted_iota(jnp.int32, (half_size, half_size), 0)
    col_index = lax.broadcasted_iota(jnp.int32, (half_size, half_size), 1)
    shifted = jnp.roll(along_col, 1)
    vertical = jnp.where(row_index == col_index, (along_col + shifted)[None, :], 0.0)
    vertical = vertical - jnp.where(
        col_index == (row_index + 1) % half_size, along_col[:, None], 0.0
    )
    vertical = vertical - jnp.where(
        row_index == (col_index + 1) % half_size, along_col[None, :], 0.0
    )
    across_diag = jnp.where(row_index == col_index, across_col[None, :], 0.0)
    upper_rows = jnp.concatenate([vertical + across_diag, -across_diag], axis=1)
    lower_rows = jnp.concatenate([-across_diag, across_diag], axis=1)
    return jnp.concatenate([upper_rows, lower_rows], axis=0)


def quarters(full_map):
    half_size = full_map.shape[0] // 2
    return (
        full_map[:half_size, :half_size],
        full_map[:half_size, half_size:],
        full_map[half_size:, :half_size],
        full_map[half_size:, half_size:],
    )


def blocked_factor(matrix):
    size_total = matrix.shape[0]
    panel = 128
    columns = []
    remaining = matrix
    for start in range(0, size_total, panel):
        head = remaining[:panel, :panel]
        head_factor = jnp.linalg.cholesky(head)
        if remaining.shape[0] > panel:
            below = remaining[panel:, :panel]
            below_factor = lax.linalg.triangular_solve(
                head_factor, below, left_side=False, lower=True, transpose_a=True
            )
            remaining = remaining[panel:, panel:] - lax.dot_general(
                below_factor,
                below_factor,
                (((1,), (1,)), ((), ())),
                precision=lax.Precision.HIGHEST,
            )
            block_column = jnp.concatenate([head_factor, below_factor], axis=0)
        else:
            block_column = head_factor
        if start > 0:
            block_column = jnp.concatenate(
                [jnp.zeros((start, panel), matrix.dtype), block_column], axis=0
            )
        columns.append(block_column)
    return jnp.concatenate(columns, axis=1)


def merge_blocks(
    left_upper, left_lower_left, left_lower, right_upper, right_upper_right, right_lower
):
    half_size = left_upper.shape[0]
    factor = blocked_factor(left_lower + right_upper)
    coupled = jnp.concatenate([left_lower_left, right_upper_right], axis=1)
    scaled = lax.linalg.triangular_solve(factor, coupled, left_side=True, lower=True)
    product = lax.dot_general(
        scaled, scaled, (((0,), (0,)), ((), ())), precision=lax.Precision.HIGHEST
    )
    zero_block = jnp.zeros((half_size, half_size), left_upper.dtype)
    diagonal_part = jnp.concatenate(
        [
            jnp.concatenate([left_upper, zero_block], axis=1),
            jnp.concatenate([zero_block, right_lower], axis=1),
        ],
        axis=0,
    )
    return diagonal_part - product


def merge_maps(left_map, right_map):
    left_upper, left_upper_right, left_lower_left, left_lower = quarters(left_map)
    right_upper, right_upper_right, right_lower_left, right_lower = quarters(right_map)
    return merge_blocks(
        left_upper, left_lower_left, left_lower, right_upper, right_upper_right, right_lower
    )


def level_payload(merged, is_right):
    upper, upper_right, lower_left, lower = quarters(merged)
    middle = jnp.where(is_right, upper_right, lower_left)
    payload = jnp.stack([upper, middle, lower])
    return payload


def joined(merged, received, is_right):
    upper, upper_right, lower_left, lower = quarters(merged)
    partner_upper = received[0]
    partner_middle = received[1]
    partner_lower = received[2]
    left_upper = jnp.where(is_right, partner_upper, upper)
    left_lower_left = jnp.where(is_right, partner_middle, lower_left)
    left_lower = jnp.where(is_right, partner_lower, lower)
    right_upper = jnp.where(is_right, upper, partner_upper)
    right_upper_right = jnp.where(is_right, upper_right, partner_middle)
    right_lower = jnp.where(is_right, lower, partner_lower)
    return merge_blocks(
        left_upper, left_lower_left, left_lower, right_upper, right_upper_right, right_lower
    )


def local_columns(classes, across_coeff, along_coeff):
    across = lookup(classes, across_coeff)
    along = lookup(classes, along_coeff)
    own_map = piece_map(across, along)
    col_levels = lax.axis_size("col").bit_length() - 1
    slab_levels = lax.axis_size("slab").bit_length() - 1
    merged = own_map
    for height in range(col_levels):
        is_right = lax.axis_index("col") >> height & 1 == 1
        received = swapped(level_payload(merged, is_right), "col", height)
        merged = joined(merged, received, is_right)
    for height in range(slab_levels):
        is_right = lax.axis_index("slab") >> height & 1 == 1
        received = swapped(level_payload(merged, is_right), "slab", height)
        merged = joined(merged, received, is_right)
    share_rows = merged.shape[0] // lax.axis_size(("slab", "col"))
    root_rows = lax.dynamic_slice_in_dim(
        merged, lax.axis_index(("slab", "col")) * share_rows, share_rows, 0
    )
    return (own_map, root_rows)


def sweep_kernel(count, size, x_ref, o_ref):
    group = min(count, 4)
    sub = lax.broadcasted_iota(jnp.int32, (1, size, size), 1)
    lane = lax.broadcasted_iota(jnp.int32, (1, 1, size), 2)

    def one(start):
        a = x_ref[pl.ds(start, group)]
        for k in range(size):
            row = a[:, k : k + 1, :]
            col = a[:, :, k : k + 1]
            inv = 1.0 / row[:, :, k : k + 1]
            scaled = jnp.where(lane == k, inv, row * inv)
            rest = jnp.where(lane == k, 0.0, a) - col * scaled
            a = jnp.where(sub == k, scaled, rest)
        o_ref[pl.ds(start, group)] = a

    if count == group:
        one(0)
    else:
        pl.loop(0, count // group)(lambda g: one(g * group))


def inverses(blocks):
    count, size, _ = blocks.shape
    return pl.pallas_call(
        functools.partial(sweep_kernel, count, size),
        out_shape=jax.ShapeDtypeStruct(blocks.shape, jnp.float32),
        in_specs=[pl.BlockSpec(memory_space=pltpu.VMEM)],
        out_specs=pl.BlockSpec(memory_space=pltpu.VMEM),
    )(blocks)


def piece_kernel(size, rows, vec_ref, cols_ref, o_ref, coef):
    levels = size.bit_length() - 1
    i = pl.program_id(0)

    def back(x, s):
        return pltpu.roll(x, s, 1)

    def fore(x, s):
        return pltpu.roll(x, size - s, 1)

    @pl.when(i == 0)
    def _():
        def wide(k):
            return jnp.broadcast_to(vec_ref[k : k + 1, :], (8, size))

        a0, a1, al0, al1 = wide(0), wide(1), wide(2), wide(3)
        sh1 = back(al1, 1)
        diag = a0 + a1 + al1 + sh1
        inv = 1.0 / diag
        coef[0] = inv
        lo = -sh1 * inv
        hi = -al1 * inv
        for level in range(levels - 1):
            s = 1 << level
            fix = 1.0 / (1.0 - lo * back(hi, s) - hi * fore(lo, s))
            coef[3 * level + 1] = -lo
            coef[3 * level + 2] = -hi
            coef[3 * level + 3] = fix
            lo, hi = -lo * back(lo, s) * fix, -hi * fore(hi, s) * fix
        g = lo + hi
        h = back(g, size // 2)
        coef[3 * levels - 2] = -g
        coef[3 * levels - 1] = 1.0 / (1.0 - g * h)

    def co(k):
        return coef[k, 0:1, :]

    row = lax.broadcasted_iota(jnp.int32, (rows, size), 0) + i * rows
    col = lax.broadcasted_iota(jnp.int32, (rows, size), 1)
    x = jnp.where(row == col, co(0), 0.0)
    for level in range(levels - 1):
        s = 1 << level
        x = (x + co(3 * level + 1) * back(x, s) + co(3 * level + 2) * fore(x, s)) * co(3 * level + 3)
    x = (x + co(3 * levels - 2) * back(x, size // 2)) * co(3 * levels - 1)
    a0, a1, al0 = vec_ref[0:1, :], vec_ref[1:2, :], vec_ref[2:3, :]
    sh0 = jnp.broadcast_to(vec_ref[4:5, :], (1, size))
    r0, r1 = cols_ref[:, 0:1], cols_ref[:, 1:2]
    vert = jnp.where(row == col, al0 + sh0 + a0, 0.0)
    vert = vert - jnp.where(row == jnp.where(col == size - 1, 0, col + 1), al0, 0.0)
    vert = vert - jnp.where(col == jnp.where(row == size - 1, 0, row + 1), sh0, 0.0)
    x0, x1 = x * a0, x * a1
    o_ref[0, :, :size] = vert - r0 * x0
    o_ref[0, :, size:] = -(r0 * x1)
    o_ref[1, :, :size] = -(r1 * x0)
    o_ref[1, :, size:] = jnp.where(row == col, a1, 0.0) - r1 * x1


def piece_map(across, along):
    size = across.shape[1]
    rows = 32
    vecs = jnp.concatenate([across, along, jnp.roll(along, 1, axis=1), along], axis=0)
    out = pl.pallas_call(
        functools.partial(piece_kernel, size, rows),
        grid=(size // rows,),
        out_shape=jax.ShapeDtypeStruct((2, size, 2 * size), jnp.float32),
        in_specs=[
            pl.BlockSpec((8, size), lambda i: (0, 0)),
            pl.BlockSpec((rows, 2), lambda i: (i, 0)),
        ],
        out_specs=pl.BlockSpec((2, rows, 2 * size), lambda i: (0, i, 0)),
        scratch_shapes=[pltpu.VMEM((3 * (size.bit_length() - 1), 8, size), jnp.float32)],
    )(vecs, across.T)
    return out.reshape(2 * size, 2 * size)


def gather_kernel(slabs, cols, x_ref, o_ref, send, recv, pass_send, pass_recv, own):
    half = cols // 2
    pairs = slabs * half
    slab, col = lax.axis_index("slab"), lax.axis_index("col")
    pair, odd = slab * half + col // 2, lax.rem(col, 2)
    me = slab * cols + col

    def place(q, side):
        return {"slab": q // half, "col": lax.rem(q, half) * 2 + side}

    def index(q, side):
        return q * 2 + side

    def to(step):
        return lax.rem(pair + step, pairs)

    def copy(src, at, sems, step, device):
        return pltpu.make_async_remote_copy(
            src_ref=src,
            dst_ref=o_ref.at[at],
            send_sem=sems[0].at[step],
            recv_sem=sems[1].at[step],
            device_id=device,
            device_id_type=pl.DeviceIdType.MESH,
        )

    barrier = pltpu.get_barrier_semaphore()
    sibling = place(pair, 1 - odd)
    for step in range(1, pairs):
        pl.semaphore_signal(
            barrier, inc=1, device_id=place(to(step), odd), device_id_type=pl.DeviceIdType.MESH
        )
    pl.semaphore_signal(barrier, inc=1, device_id=sibling, device_id_type=pl.DeviceIdType.MESH)
    pl.semaphore_wait(barrier, pairs)

    local_copy = pltpu.make_async_copy(x_ref, o_ref.at[me], own)
    local_copy.start()
    out = [copy(x_ref, me, (send, recv), step, place(to(step), odd)) for step in range(1, pairs)]
    for c in out:
        c.start()
    passed = [copy(x_ref, me, (pass_send, pass_recv), 0, sibling)]
    passed[0].start()
    for step in range(1, pairs):
        at = index(to(pairs - step), odd)
        copy(x_ref, at, (send, recv), step, sibling).wait_recv()
        c = copy(o_ref.at[at], at, (pass_send, pass_recv), step, sibling)
        c.start()
        passed.append(c)
    for step in range(pairs):
        at = index(to(pairs - step), 1 - odd)
        copy(x_ref, at, (pass_send, pass_recv), step, sibling).wait_recv()
    for c in out + passed:
        c.wait_send()
    local_copy.wait()


def gathered(block, number):
    slabs, cols = lax.axis_size("slab"), lax.axis_size("col")
    if cols % 2:
        return lax.all_gather(block, AXES, axis=0)
    pairs = slabs * cols // 2
    return pl.pallas_call(
        functools.partial(gather_kernel, slabs, cols),
        out_shape=jax.ShapeDtypeStruct((slabs * cols,) + block.shape, block.dtype),
        in_specs=[pl.BlockSpec(memory_space=pltpu.VMEM)],
        out_specs=pl.BlockSpec(memory_space=pltpu.VMEM),
        scratch_shapes=[pltpu.SemaphoreType.DMA((pairs,))] * 4 + [pltpu.SemaphoreType.DMA],
        compiler_params=pltpu.CompilerParams(collective_id=number, has_side_effects=True),
    )(block)


def bmm(a, b):
    return jnp.einsum("bij,bjk->bik", a, b, precision=HIGHEST)


def bmm_t(a, b):
    return jnp.einsum("bji,bjk->bik", a, b, precision=HIGHEST)


def t(a):
    return jnp.swapaxes(a, 1, 2)


def row_elements(across, along_prev, along):
    rows, cols = across.shape
    spot = lax.broadcasted_iota(jnp.int32, (rows, cols), 1)
    inner = spot > 0
    diag = jnp.where(inner, jnp.roll(across, 1, axis=1) + across + along_prev + along, 1.0)
    off = jnp.where(inner, across, 0.0)
    i = lax.broadcasted_iota(jnp.int32, (1, cols, cols), 1)
    j = lax.broadcasted_iota(jnp.int32, (1, cols, cols), 2)
    bb = jnp.where(i == j, diag[:, :, None], 0.0)
    bb = bb - jnp.where(j == i + 1, off[:, :, None], 0.0) - jnp.where(i == j + 1, off[:, None, :], 0.0)
    tb = jnp.where(i == j, -jnp.where(inner, along_prev, 0.0)[:, :, None], 0.0)
    tt = jnp.zeros_like(bb)
    first = jnp.where(spot == 1, -across[:, :1], 0.0)
    last = jnp.where(spot == cols - 1, -across[:, cols - 1 :], 0.0)
    fb = jnp.stack([first, last], axis=2)
    return tt, tb, bb, jnp.zeros_like(fb), fb, jnp.zeros((rows, 2, 2), jnp.float32)


def merge_elements(parts):
    (tta, ttb), (tba, tbb), (bba, bbb), (fta, ftb), (fba, fbb), (kka, kkb) = [
        (p[0::2], p[1::2]) for p in parts
    ]
    n, k = tta.shape[1], fta.shape[2]
    w = jnp.concatenate([t(tba), tbb, fba, ftb], axis=2)
    z = bmm(inverses(bba + ttb), w)
    u = bmm_t(w, z)
    zero = jnp.zeros_like(fta)
    zk = jnp.zeros_like(kka)
    kk = jnp.concatenate(
        [jnp.concatenate([kka, zk], axis=2), jnp.concatenate([zk, kkb], axis=2)], axis=1
    )
    return (
        tta - u[:, :n, :n],
        -u[:, :n, n : 2 * n],
        bbb - u[:, n : 2 * n, n : 2 * n],
        jnp.concatenate([fta, zero], axis=2) - u[:, :n, 2 * n :],
        jnp.concatenate([zero, fbb], axis=2) - u[:, n : 2 * n, 2 * n :],
        kk - u[:, 2 * n :, 2 * n :],
    )


def ring_solve(d, link, rhs):
    count, n = d.shape[0], d.shape[1]
    if count == 1:
        return bmm(inverses(d + link + t(link)), rhs)
    w = jnp.concatenate([t(link[0::2]), link[1::2], rhs[0::2]], axis=2)
    z = bmm(inverses(d[0::2]), w)
    u = bmm_t(w[:, :, : 2 * n], z)
    after = jnp.roll(u, -1, axis=0)
    d_next = d[1::2] - u[:, n:, n : 2 * n] - after[:, :n, :n]
    r_next = rhs[1::2] - u[:, n:, 2 * n :] - after[:, :n, 2 * n :]
    odd = ring_solve(d_next, -u[:, :n, n : 2 * n], r_next)
    both = jnp.concatenate([jnp.roll(odd, 1, axis=0), odd], axis=1)
    even = z[:, :, 2 * n :] - bmm(z[:, :, : 2 * n], both)
    return jnp.stack([even, odd], axis=1).reshape(rhs.shape)


def local_rows(classes, across_coeff, along_coeff):
    own_across = lookup(classes, across_coeff)
    own_along = lookup(classes, along_coeff)
    devices = lax.axis_size(AXES)
    me = lax.axis_index(AXES)
    size = classes.shape[1]
    cols = classes.shape[0] * devices
    height = size // devices
    everyone = gathered(classes, 0).reshape(cols, size)
    own_map = piece_map(own_across, own_along)
    padded = jnp.concatenate([everyone[:, size - 1 :], everyone], axis=1)
    mine = lax.dynamic_slice_in_dim(padded, me * height, height + 1, 1)
    across = lookup(mine, across_coeff).T
    along = lookup(mine, along_coeff).T
    parts = row_elements(across[1:], along[:-1], along[1:])
    while parts[0].shape[0] > 1:
        parts = merge_elements(parts)
    tt, tb, bb, ft, fb, kk = [p[0] for p in parts]

    def sides(f):
        return f.reshape(f.shape[0], height, 2).swapaxes(1, 2).reshape(f.shape[0], 2 * height)

    ft, fb = sides(ft), sides(fb)
    kk = sides(sides(kk).T)
    wide = jnp.concatenate(
        [jnp.concatenate([tt, tb], axis=1), jnp.concatenate([bb, ft, fb], axis=1)], axis=0
    )
    lanes = wide.shape[1]
    kk_rows = kk.size // lanes
    wide = jnp.concatenate([wide, kk.reshape(kk_rows, lanes)], axis=0)
    wide = gathered(wide, 1)
    top, low = wide[:, :cols], wide[:, cols : 2 * cols]
    k = 2 * height
    tt, tb = top[:, :, :cols], top[:, :, cols:]
    bb, ft, fb = low[:, :, :cols], low[:, :, cols : cols + k], low[:, :, cols + k :]
    kk = wide[:, 2 * cols :].reshape(devices, k, k)
    share = 2 * size // devices
    start = me * share
    side = start // size
    r0 = start - side * size
    s0 = r0 // height
    strip = lax.broadcasted_iota(jnp.int32, (devices, 1, 1), 0)

    def cut(f, a):
        return lax.dynamic_slice(f, (s0 + a, 0, side * height), (1, f.shape[1], height))[0]

    def at(f, a):
        return jnp.where(strip == s0 + a, f[None], 0.0)

    def rhs_of(f):
        return jnp.concatenate([at(cut(f, 0), 0), at(cut(f, 1), 1)], axis=2)

    rhs = rhs_of(fb) + jnp.roll(rhs_of(ft), -1, axis=0)
    x = ring_solve(bb + jnp.roll(tt, -1, axis=0), tb, rhs)
    x = jnp.concatenate([jnp.roll(x, 1, axis=0), x], axis=1)
    f = jnp.concatenate([ft, fb], axis=1)
    k_rows = jnp.concatenate([at(cut(kk, 0).T, 0), at(cut(kk, 1).T, 1)], axis=1)
    rows = k_rows - bmm_t(x, f)
    rows = rows.reshape(devices, share, 2, height).transpose(1, 2, 0, 3).reshape(share, 2 * size)

    first_ac = lookup(everyone[:1], across_coeff)
    last_ac = lookup(everyone[cols - 1 :], across_coeff)
    al = lookup(everyone[:1], along_coeff)
    sh = jnp.roll(al, 1, axis=1)
    zero = jnp.zeros_like(al)
    on = jnp.concatenate([first_ac + al + sh, last_ac], axis=1)
    below = jnp.concatenate([al, zero], axis=1)
    above = jnp.concatenate([sh, zero], axis=1)
    row = lax.broadcasted_iota(jnp.int32, (share, 2 * size), 0) + start
    col = lax.broadcasted_iota(jnp.int32, (share, 2 * size), 1)
    rows = rows + jnp.where(row == col, on, 0.0)
    rows = rows - jnp.where((row == (col + 1) % size) & (row < size) & (col < size), below, 0.0)
    rows = rows - jnp.where((col == (row + 1) % size) & (row < size) & (col < size), above, 0.0)
    return own_map, rows


def local(classes, across_coeff, along_coeff):
    devices = lax.axis_size(AXES)
    cols = classes.shape[0] * devices
    if 4 * cols <= classes.shape[1] and 4 * classes.shape[1] == cols * devices:
        return local_rows(classes, across_coeff, along_coeff)
    return local_columns(classes, across_coeff, along_coeff)


def solution(mesh):
    placed = (P(("slab", "col"), None), P(), P())
    return jax.shard_map(
        local,
        mesh=mesh,
        in_specs=placed,
        out_specs=(P(("slab", "col"), None), P(("slab", "col"), None)),
        check_vma=False,
    )
```

```python
import functools
import jax
import jax.numpy as jnp
from jax import lax
from jax.experimental import pallas as pl
from jax.experimental.pallas import tpu as pltpu
from jax.sharding import PartitionSpec as P

PRODUCT = lax.Precision.HIGH
AXES = ("slab", "col")


def swapped(block, axis, stride):
    count = lax.axis_size(axis)
    route = []
    for low in range(count):
        high = low | 1 << stride
        if high != low and high < count:
            route += [(low, high), (high, low)]
    return lax.ppermute(block, axis, route)


def lookup(classes, values_table):
    levels = jnp.arange(values_table.shape[0], dtype=jnp.int32)
    matches = classes[:, None, :] == levels[None, :, None]
    return jnp.sum(jnp.where(matches, values_table[None, :, None], 0.0), axis=1)


def strip_map(along_col, across_col):
    half_size = along_col.shape[0]
    row_index = lax.broadcasted_iota(jnp.int32, (half_size, half_size), 0)
    col_index = lax.broadcasted_iota(jnp.int32, (half_size, half_size), 1)
    shifted = jnp.roll(along_col, 1)
    vertical = jnp.where(row_index == col_index, (along_col + shifted)[None, :], 0.0)
    vertical = vertical - jnp.where(
        col_index == (row_index + 1) % half_size, along_col[:, None], 0.0
    )
    vertical = vertical - jnp.where(
        row_index == (col_index + 1) % half_size, along_col[None, :], 0.0
    )
    across_diag = jnp.where(row_index == col_index, across_col[None, :], 0.0)
    upper_rows = jnp.concatenate([vertical + across_diag, -across_diag], axis=1)
    lower_rows = jnp.concatenate([-across_diag, across_diag], axis=1)
    return jnp.concatenate([upper_rows, lower_rows], axis=0)


def quarters(full_map):
    half_size = full_map.shape[0] // 2
    return (
        full_map[:half_size, :half_size],
        full_map[:half_size, half_size:],
        full_map[half_size:, :half_size],
        full_map[half_size:, half_size:],
    )


def blocked_factor(matrix):
    size_total = matrix.shape[0]
    panel = 128
    columns = []
    remaining = matrix
    for start in range(0, size_total, panel):
        head = remaining[:panel, :panel]
        head_factor = jnp.linalg.cholesky(head)
        if remaining.shape[0] > panel:
            below = remaining[panel:, :panel]
            below_factor = lax.linalg.triangular_solve(
                head_factor, below, left_side=False, lower=True, transpose_a=True
            )
            remaining = remaining[panel:, panel:] - lax.dot_general(
                below_factor,
                below_factor,
                (((1,), (1,)), ((), ())),
                precision=lax.Precision.HIGHEST,
            )
            block_column = jnp.concatenate([head_factor, below_factor], axis=0)
        else:
            block_column = head_factor
        if start > 0:
            block_column = jnp.concatenate(
                [jnp.zeros((start, panel), matrix.dtype), block_column], axis=0
            )
        columns.append(block_column)
    return jnp.concatenate(columns, axis=1)


def merge_blocks(
    left_upper, left_lower_left, left_lower, right_upper, right_upper_right, right_lower
):
    half_size = left_upper.shape[0]
    factor = blocked_factor(left_lower + right_upper)
    coupled = jnp.concatenate([left_lower_left, right_upper_right], axis=1)
    scaled = lax.linalg.triangular_solve(factor, coupled, left_side=True, lower=True)
    product = lax.dot_general(
        scaled, scaled, (((0,), (0,)), ((), ())), precision=lax.Precision.HIGHEST
    )
    zero_block = jnp.zeros((half_size, half_size), left_upper.dtype)
    diagonal_part = jnp.concatenate(
        [
            jnp.concatenate([left_upper, zero_block], axis=1),
            jnp.concatenate([zero_block, right_lower], axis=1),
        ],
        axis=0,
    )
    return diagonal_part - product


def merge_maps(left_map, right_map):
    left_upper, left_upper_right, left_lower_left, left_lower = quarters(left_map)
    right_upper, right_upper_right, right_lower_left, right_lower = quarters(right_map)
    return merge_blocks(
        left_upper, left_lower_left, left_lower, right_upper, right_upper_right, right_lower
    )


def level_payload(merged, is_right):
    upper, upper_right, lower_left, lower = quarters(merged)
    middle = jnp.where(is_right, upper_right, lower_left)
    payload = jnp.stack([upper, middle, lower])
    return payload


def joined(merged, received, is_right):
    upper, upper_right, lower_left, lower = quarters(merged)
    partner_upper = received[0]
    partner_middle = received[1]
    partner_lower = received[2]
    left_upper = jnp.where(is_right, partner_upper, upper)
    left_lower_left = jnp.where(is_right, partner_middle, lower_left)
    left_lower = jnp.where(is_right, partner_lower, lower)
    right_upper = jnp.where(is_right, upper, partner_upper)
    right_upper_right = jnp.where(is_right, upper_right, partner_middle)
    right_lower = jnp.where(is_right, lower, partner_lower)
    return merge_blocks(
        left_upper, left_lower_left, left_lower, right_upper, right_upper_right, right_lower
    )


def local_columns(classes, across_coeff, along_coeff):
    across = lookup(classes, across_coeff)
    along = lookup(classes, along_coeff)
    own_map = piece_map(across, along)
    col_levels = lax.axis_size("col").bit_length() - 1
    slab_levels = lax.axis_size("slab").bit_length() - 1
    merged = own_map
    for height in range(col_levels):
        is_right = lax.axis_index("col") >> height & 1 == 1
        received = swapped(level_payload(merged, is_right), "col", height)
        merged = joined(merged, received, is_right)
    for height in range(slab_levels):
        is_right = lax.axis_index("slab") >> height & 1 == 1
        received = swapped(level_payload(merged, is_right), "slab", height)
        merged = joined(merged, received, is_right)
    share_rows = merged.shape[0] // lax.axis_size(("slab", "col"))
    root_rows = lax.dynamic_slice_in_dim(
        merged, lax.axis_index(("slab", "col")) * share_rows, share_rows, 0
    )
    return (own_map, root_rows)


GROUP = 16


def sweep_kernel(count, size, x_ref, o_ref):
    group = min(count, GROUP)
    sub = lax.broadcasted_iota(jnp.int32, (1, size, size), 1)
    lane = lax.broadcasted_iota(jnp.int32, (1, 1, size), 2)

    def one(start):
        a = x_ref[pl.ds(start, group)]
        for k in range(0, size, 2):
            row0, row1 = a[:, k : k + 1, :], a[:, k + 1 : k + 2, :]
            col0, col1 = a[:, :, k : k + 1], a[:, :, k + 1 : k + 2]
            p, q, r = row0[:, :, k : k + 1], row0[:, :, k + 1 : k + 2], row1[:, :, k + 1 : k + 2]
            inv = 1.0 / (p * r - q * q)
            is0, is1 = lane == k, lane == k + 1
            row0 = jnp.where(is0, 1.0, jnp.where(is1, 0.0, row0))
            row1 = jnp.where(is0, 0.0, jnp.where(is1, 1.0, row1))
            s0 = (r * row0 - q * row1) * inv
            s1 = (p * row1 - q * row0) * inv
            rest = jnp.where(is0 | is1, 0.0, a) - col0 * s0 - col1 * s1
            a = jnp.where(sub == k, s0, jnp.where(sub == k + 1, s1, rest))
        o_ref[pl.ds(start, group)] = a

    if count == group:
        one(0)
    else:
        pl.loop(0, count // group)(lambda g: one(g * group))


def inverses(blocks):
    count, size, _ = blocks.shape
    return pl.pallas_call(
        functools.partial(sweep_kernel, count, size),
        out_shape=jax.ShapeDtypeStruct(blocks.shape, jnp.float32),
        in_specs=[pl.BlockSpec(memory_space=pltpu.VMEM)],
        out_specs=pl.BlockSpec(memory_space=pltpu.VMEM),
    )(blocks)


def piece_kernel(size, rows, vec_ref, cols_ref, o_ref, coef):
    levels = size.bit_length() - 1
    i = pl.program_id(0)

    def back(x, s):
        return pltpu.roll(x, s, 1)

    def fore(x, s):
        return pltpu.roll(x, size - s, 1)

    @pl.when(i == 0)
    def _():
        def wide(k):
            return jnp.broadcast_to(vec_ref[k : k + 1, :], (8, size))

        a0, a1, al0, al1 = wide(0), wide(1), wide(2), wide(3)
        sh1 = back(al1, 1)
        diag = a0 + a1 + al1 + sh1
        inv = 1.0 / diag
        coef[0] = inv
        lo = -sh1 * inv
        hi = -al1 * inv
        for level in range(levels - 1):
            s = 1 << level
            fix = 1.0 / (1.0 - lo * back(hi, s) - hi * fore(lo, s))
            coef[3 * level + 1] = -lo
            coef[3 * level + 2] = -hi
            coef[3 * level + 3] = fix
            lo, hi = -lo * back(lo, s) * fix, -hi * fore(hi, s) * fix
        g = lo + hi
        h = back(g, size // 2)
        coef[3 * levels - 2] = -g
        coef[3 * levels - 1] = 1.0 / (1.0 - g * h)

    def co(k):
        return coef[k, 0:1, :]

    row = lax.broadcasted_iota(jnp.int32, (rows, size), 0) + i * rows
    col = lax.broadcasted_iota(jnp.int32, (rows, size), 1)
    x = jnp.where(row == col, co(0), 0.0)
    for level in range(levels - 1):
        s = 1 << level
        x = (x + co(3 * level + 1) * back(x, s) + co(3 * level + 2) * fore(x, s)) * co(3 * level + 3)
    x = (x + co(3 * levels - 2) * back(x, size // 2)) * co(3 * levels - 1)
    a0, a1, al0 = vec_ref[0:1, :], vec_ref[1:2, :], vec_ref[2:3, :]
    sh0 = jnp.broadcast_to(vec_ref[4:5, :], (1, size))
    r0, r1 = cols_ref[:, 0:1], cols_ref[:, 1:2]
    vert = jnp.where(row == col, al0 + sh0 + a0, 0.0)
    vert = vert - jnp.where(row == jnp.where(col == size - 1, 0, col + 1), al0, 0.0)
    vert = vert - jnp.where(col == jnp.where(row == size - 1, 0, row + 1), sh0, 0.0)
    x0, x1 = x * a0, x * a1
    o_ref[0, :, :size] = vert - r0 * x0
    o_ref[0, :, size:] = -(r0 * x1)
    o_ref[1, :, :size] = -(r1 * x0)
    o_ref[1, :, size:] = jnp.where(row == col, a1, 0.0) - r1 * x1


def piece_map(across, along):
    size = across.shape[1]
    rows = 32
    vecs = jnp.concatenate([across, along, jnp.roll(along, 1, axis=1), along], axis=0)
    out = pl.pallas_call(
        functools.partial(piece_kernel, size, rows),
        grid=(size // rows,),
        out_shape=jax.ShapeDtypeStruct((2, size, 2 * size), jnp.float32),
        in_specs=[
            pl.BlockSpec((8, size), lambda i: (0, 0)),
            pl.BlockSpec((rows, 2), lambda i: (i, 0)),
        ],
        out_specs=pl.BlockSpec((2, rows, 2 * size), lambda i: (0, i, 0)),
        scratch_shapes=[pltpu.VMEM((3 * (size.bit_length() - 1), 8, size), jnp.float32)],
    )(vecs, across.T)
    return out.reshape(2 * size, 2 * size)


def gather_kernel(slabs, cols, x_ref, o_ref, send, recv, pass_send, pass_recv, own):
    half = cols // 2
    pairs = slabs * half
    slab, col = lax.axis_index("slab"), lax.axis_index("col")
    pair, odd = slab * half + col // 2, lax.rem(col, 2)
    me = slab * cols + col

    def place(q, side):
        return {"slab": q // half, "col": lax.rem(q, half) * 2 + side}

    def index(q, side):
        return q * 2 + side

    def to(step):
        return lax.rem(pair + step, pairs)

    def copy(src, at, sems, step, device):
        return pltpu.make_async_remote_copy(
            src_ref=src,
            dst_ref=o_ref.at[at],
            send_sem=sems[0].at[step],
            recv_sem=sems[1].at[step],
            device_id=device,
            device_id_type=pl.DeviceIdType.MESH,
        )

    barrier = pltpu.get_barrier_semaphore()
    sibling = place(pair, 1 - odd)
    for step in range(1, pairs):
        pl.semaphore_signal(
            barrier, inc=1, device_id=place(to(step), odd), device_id_type=pl.DeviceIdType.MESH
        )
    pl.semaphore_signal(barrier, inc=1, device_id=sibling, device_id_type=pl.DeviceIdType.MESH)
    pl.semaphore_wait(barrier, pairs)

    local_copy = pltpu.make_async_copy(x_ref, o_ref.at[me], own)
    local_copy.start()
    out = [copy(x_ref, me, (send, recv), step, place(to(step), odd)) for step in range(1, pairs)]
    for c in out:
        c.start()
    passed = [copy(x_ref, me, (pass_send, pass_recv), 0, sibling)]
    passed[0].start()
    for step in range(1, pairs):
        at = index(to(pairs - step), odd)
        copy(x_ref, at, (send, recv), step, sibling).wait_recv()
        c = copy(o_ref.at[at], at, (pass_send, pass_recv), step, sibling)
        c.start()
        passed.append(c)
    for step in range(pairs):
        at = index(to(pairs - step), 1 - odd)
        copy(x_ref, at, (pass_send, pass_recv), step, sibling).wait_recv()
    for c in out + passed:
        c.wait_send()
    local_copy.wait()


def gathered(block, number):
    slabs, cols = lax.axis_size("slab"), lax.axis_size("col")
    if cols % 2:
        return lax.all_gather(block, AXES, axis=0)
    pairs = slabs * cols // 2
    return pl.pallas_call(
        functools.partial(gather_kernel, slabs, cols),
        out_shape=jax.ShapeDtypeStruct((slabs * cols,) + block.shape, block.dtype),
        in_specs=[pl.BlockSpec(memory_space=pltpu.VMEM)],
        out_specs=pl.BlockSpec(memory_space=pltpu.VMEM),
        scratch_shapes=[pltpu.SemaphoreType.DMA((pairs,))] * 4 + [pltpu.SemaphoreType.DMA],
        compiler_params=pltpu.CompilerParams(collective_id=number, has_side_effects=True),
    )(block)


def bmm(a, b):
    return jnp.einsum("bij,bjk->bik", a, b, precision=PRODUCT)


def bmm_t(a, b):
    return jnp.einsum("bji,bjk->bik", a, b, precision=PRODUCT)


def t(a):
    return jnp.swapaxes(a, 1, 2)


def row_elements(across, along_prev, along):
    rows, cols = across.shape
    spot = lax.broadcasted_iota(jnp.int32, (rows, cols), 1)
    inner = spot > 0
    diag = jnp.where(inner, jnp.roll(across, 1, axis=1) + across + along_prev + along, 1.0)
    off = jnp.where(inner, across, 0.0)
    i = lax.broadcasted_iota(jnp.int32, (1, cols, cols), 1)
    j = lax.broadcasted_iota(jnp.int32, (1, cols, cols), 2)
    bb = jnp.where(i == j, diag[:, :, None], 0.0)
    bb = bb - jnp.where(j == i + 1, off[:, :, None], 0.0) - jnp.where(i == j + 1, off[:, None, :], 0.0)
    tb = jnp.where(i == j, -jnp.where(inner, along_prev, 0.0)[:, :, None], 0.0)
    tt = jnp.zeros_like(bb)
    first = jnp.where(spot == 1, -across[:, :1], 0.0)
    last = jnp.where(spot == cols - 1, -across[:, cols - 1 :], 0.0)
    fb = jnp.stack([first, last], axis=2)
    return tt, tb, bb, jnp.zeros_like(fb), fb, jnp.zeros((rows, 2, 2), jnp.float32)


def merge_elements(parts):
    (tta, ttb), (tba, tbb), (bba, bbb), (fta, ftb), (fba, fbb), (kka, kkb) = [
        (p[0::2], p[1::2]) for p in parts
    ]
    n, k = tta.shape[1], fta.shape[2]
    w = jnp.concatenate([t(tba), tbb, fba, ftb], axis=2)
    z = bmm(inverses(bba + ttb), w)
    u = bmm_t(w, z)
    zero = jnp.zeros_like(fta)
    zk = jnp.zeros_like(kka)
    kk = jnp.concatenate(
        [jnp.concatenate([kka, zk], axis=2), jnp.concatenate([zk, kkb], axis=2)], axis=1
    )
    return (
        tta - u[:, :n, :n],
        -u[:, :n, n : 2 * n],
        bbb - u[:, n : 2 * n, n : 2 * n],
        jnp.concatenate([fta, zero], axis=2) - u[:, :n, 2 * n :],
        jnp.concatenate([zero, fbb], axis=2) - u[:, n : 2 * n, 2 * n :],
        kk - u[:, 2 * n :, 2 * n :],
    )


def ring_solve(d, link, rhs):
    count, n = d.shape[0], d.shape[1]
    if count == 1:
        return bmm(inverses(d + link + t(link)), rhs)
    w = jnp.concatenate([t(link[0::2]), link[1::2], rhs[0::2]], axis=2)
    z = bmm(inverses(d[0::2]), w)
    u = bmm_t(w[:, :, : 2 * n], z)
    after = jnp.roll(u, -1, axis=0)
    d_next = d[1::2] - u[:, n:, n : 2 * n] - after[:, :n, :n]
    r_next = rhs[1::2] - u[:, n:, 2 * n :] - after[:, :n, 2 * n :]
    odd = ring_solve(d_next, -u[:, :n, n : 2 * n], r_next)
    both = jnp.concatenate([jnp.roll(odd, 1, axis=0), odd], axis=1)
    even = z[:, :, 2 * n :] - bmm(z[:, :, : 2 * n], both)
    return jnp.stack([even, odd], axis=1).reshape(rhs.shape)


def local_rows(classes, across_coeff, along_coeff):
    own_across = lookup(classes, across_coeff)
    own_along = lookup(classes, along_coeff)
    devices = lax.axis_size(AXES)
    me = lax.axis_index(AXES)
    size = classes.shape[1]
    cols = classes.shape[0] * devices
    height = size // devices
    everyone = gathered(classes, 0).reshape(cols, size)
    own_map = piece_map(own_across, own_along)
    padded = jnp.concatenate([everyone[:, size - 1 :], everyone], axis=1)
    mine = lax.dynamic_slice_in_dim(padded, me * height, height + 1, 1)
    across = lookup(mine, across_coeff).T
    along = lookup(mine, along_coeff).T
    parts = row_elements(across[1:], along[:-1], along[1:])
    while parts[0].shape[0] > 1:
        parts = merge_elements(parts)
    tt, tb, bb, ft, fb, kk = [p[0] for p in parts]

    def sides(f):
        return f.reshape(f.shape[0], height, 2).swapaxes(1, 2).reshape(f.shape[0], 2 * height)

    ft, fb = sides(ft), sides(fb)
    kk = sides(sides(kk).T)
    wide = jnp.concatenate(
        [jnp.concatenate([tt, tb], axis=1), jnp.concatenate([bb, ft, fb], axis=1)], axis=0
    )
    lanes = wide.shape[1]
    kk_rows = kk.size // lanes
    wide = jnp.concatenate([wide, kk.reshape(kk_rows, lanes)], axis=0)
    wide = gathered(wide, 1)
    top, low = wide[:, :cols], wide[:, cols : 2 * cols]
    k = 2 * height
    tt, tb = top[:, :, :cols], top[:, :, cols:]
    bb, ft, fb = low[:, :, :cols], low[:, :, cols : cols + k], low[:, :, cols + k :]
    kk = wide[:, 2 * cols :].reshape(devices, k, k)
    share = 2 * size // devices
    start = me * share
    side = start // size
    r0 = start - side * size
    s0 = r0 // height
    strip = lax.broadcasted_iota(jnp.int32, (devices, 1, 1), 0)

    def cut(f, a):
        return lax.dynamic_slice(f, (s0 + a, 0, side * height), (1, f.shape[1], height))[0]

    def at(f, a):
        return jnp.where(strip == s0 + a, f[None], 0.0)

    def rhs_of(f):
        return jnp.concatenate([at(cut(f, 0), 0), at(cut(f, 1), 1)], axis=2)

    rhs = rhs_of(fb) + jnp.roll(rhs_of(ft), -1, axis=0)
    x = ring_solve(bb + jnp.roll(tt, -1, axis=0), tb, rhs)
    x = jnp.concatenate([jnp.roll(x, 1, axis=0), x], axis=1)
    f = jnp.concatenate([ft, fb], axis=1)
    k_rows = jnp.concatenate([at(cut(kk, 0).T, 0), at(cut(kk, 1).T, 1)], axis=1)
    rows = k_rows - bmm_t(x, f)
    rows = rows.reshape(devices, share, 2, height).transpose(1, 2, 0, 3).reshape(share, 2 * size)

    first_ac = lookup(everyone[:1], across_coeff)
    last_ac = lookup(everyone[cols - 1 :], across_coeff)
    al = lookup(everyone[:1], along_coeff)
    sh = jnp.roll(al, 1, axis=1)
    zero = jnp.zeros_like(al)
    on = jnp.concatenate([first_ac + al + sh, last_ac], axis=1)
    below = jnp.concatenate([al, zero], axis=1)
    above = jnp.concatenate([sh, zero], axis=1)
    row = lax.broadcasted_iota(jnp.int32, (share, 2 * size), 0) + start
    col = lax.broadcasted_iota(jnp.int32, (share, 2 * size), 1)
    rows = rows + jnp.where(row == col, on, 0.0)
    rows = rows - jnp.where((row == (col + 1) % size) & (row < size) & (col < size), below, 0.0)
    rows = rows - jnp.where((col == (row + 1) % size) & (row < size) & (col < size), above, 0.0)
    return own_map, rows


def local(classes, across_coeff, along_coeff):
    devices = lax.axis_size(AXES)
    cols = classes.shape[0] * devices
    if 4 * cols <= classes.shape[1] and 4 * classes.shape[1] == cols * devices:
        return local_rows(classes, across_coeff, along_coeff)
    return local_columns(classes, across_coeff, along_coeff)


def solution(mesh):
    placed = (P(("slab", "col"), None), P(), P())
    return jax.shard_map(
        local,
        mesh=mesh,
        in_specs=placed,
        out_specs=(P(("slab", "col"), None), P(("slab", "col"), None)),
        check_vma=False,
    )
```

```python
import functools
import jax
import jax.numpy as jnp
from jax import lax
from jax.experimental import pallas as pl
from jax.experimental.pallas import tpu as pltpu
from jax.sharding import PartitionSpec as P

PRODUCT = lax.Precision.HIGHEST
AXES = ("slab", "col")


def swapped(block, axis, stride):
    count = lax.axis_size(axis)
    route = []
    for low in range(count):
        high = low | 1 << stride
        if high != low and high < count:
            route += [(low, high), (high, low)]
    return lax.ppermute(block, axis, route)


def lookup(classes, values_table):
    levels = jnp.arange(values_table.shape[0], dtype=jnp.int32)
    matches = classes[:, None, :] == levels[None, :, None]
    return jnp.sum(jnp.where(matches, values_table[None, :, None], 0.0), axis=1)


def strip_map(along_col, across_col):
    half_size = along_col.shape[0]
    row_index = lax.broadcasted_iota(jnp.int32, (half_size, half_size), 0)
    col_index = lax.broadcasted_iota(jnp.int32, (half_size, half_size), 1)
    shifted = jnp.roll(along_col, 1)
    vertical = jnp.where(row_index == col_index, (along_col + shifted)[None, :], 0.0)
    vertical = vertical - jnp.where(
        col_index == (row_index + 1) % half_size, along_col[:, None], 0.0
    )
    vertical = vertical - jnp.where(
        row_index == (col_index + 1) % half_size, along_col[None, :], 0.0
    )
    across_diag = jnp.where(row_index == col_index, across_col[None, :], 0.0)
    upper_rows = jnp.concatenate([vertical + across_diag, -across_diag], axis=1)
    lower_rows = jnp.concatenate([-across_diag, across_diag], axis=1)
    return jnp.concatenate([upper_rows, lower_rows], axis=0)


def quarters(full_map):
    half_size = full_map.shape[0] // 2
    return (
        full_map[:half_size, :half_size],
        full_map[:half_size, half_size:],
        full_map[half_size:, :half_size],
        full_map[half_size:, half_size:],
    )


def blocked_factor(matrix):
    size_total = matrix.shape[0]
    panel = 128
    columns = []
    remaining = matrix
    for start in range(0, size_total, panel):
        head = remaining[:panel, :panel]
        head_factor = jnp.linalg.cholesky(head)
        if remaining.shape[0] > panel:
            below = remaining[panel:, :panel]
            below_factor = lax.linalg.triangular_solve(
                head_factor, below, left_side=False, lower=True, transpose_a=True
            )
            remaining = remaining[panel:, panel:] - lax.dot_general(
                below_factor,
                below_factor,
                (((1,), (1,)), ((), ())),
                precision=lax.Precision.HIGHEST,
            )
            block_column = jnp.concatenate([head_factor, below_factor], axis=0)
        else:
            block_column = head_factor
        if start > 0:
            block_column = jnp.concatenate(
                [jnp.zeros((start, panel), matrix.dtype), block_column], axis=0
            )
        columns.append(block_column)
    return jnp.concatenate(columns, axis=1)


def merge_blocks(
    left_upper, left_lower_left, left_lower, right_upper, right_upper_right, right_lower
):
    half_size = left_upper.shape[0]
    factor = blocked_factor(left_lower + right_upper)
    coupled = jnp.concatenate([left_lower_left, right_upper_right], axis=1)
    scaled = lax.linalg.triangular_solve(factor, coupled, left_side=True, lower=True)
    product = lax.dot_general(
        scaled, scaled, (((0,), (0,)), ((), ())), precision=lax.Precision.HIGHEST
    )
    zero_block = jnp.zeros((half_size, half_size), left_upper.dtype)
    diagonal_part = jnp.concatenate(
        [
            jnp.concatenate([left_upper, zero_block], axis=1),
            jnp.concatenate([zero_block, right_lower], axis=1),
        ],
        axis=0,
    )
    return diagonal_part - product


def merge_maps(left_map, right_map):
    left_upper, left_upper_right, left_lower_left, left_lower = quarters(left_map)
    right_upper, right_upper_right, right_lower_left, right_lower = quarters(right_map)
    return merge_blocks(
        left_upper, left_lower_left, left_lower, right_upper, right_upper_right, right_lower
    )


def level_payload(merged, is_right):
    upper, upper_right, lower_left, lower = quarters(merged)
    middle = jnp.where(is_right, upper_right, lower_left)
    payload = jnp.stack([upper, middle, lower])
    return payload


def joined(merged, received, is_right):
    upper, upper_right, lower_left, lower = quarters(merged)
    partner_upper = received[0]
    partner_middle = received[1]
    partner_lower = received[2]
    left_upper = jnp.where(is_right, partner_upper, upper)
    left_lower_left = jnp.where(is_right, partner_middle, lower_left)
    left_lower = jnp.where(is_right, partner_lower, lower)
    right_upper = jnp.where(is_right, upper, partner_upper)
    right_upper_right = jnp.where(is_right, upper_right, partner_middle)
    right_lower = jnp.where(is_right, lower, partner_lower)
    return merge_blocks(
        left_upper, left_lower_left, left_lower, right_upper, right_upper_right, right_lower
    )


def local_columns(classes, across_coeff, along_coeff):
    across = lookup(classes, across_coeff)
    along = lookup(classes, along_coeff)
    own_map = piece_map(across, along)
    col_levels = lax.axis_size("col").bit_length() - 1
    slab_levels = lax.axis_size("slab").bit_length() - 1
    merged = own_map
    for height in range(col_levels):
        is_right = lax.axis_index("col") >> height & 1 == 1
        received = swapped(level_payload(merged, is_right), "col", height)
        merged = joined(merged, received, is_right)
    for height in range(slab_levels):
        is_right = lax.axis_index("slab") >> height & 1 == 1
        received = swapped(level_payload(merged, is_right), "slab", height)
        merged = joined(merged, received, is_right)
    share_rows = merged.shape[0] // lax.axis_size(("slab", "col"))
    root_rows = lax.dynamic_slice_in_dim(
        merged, lax.axis_index(("slab", "col")) * share_rows, share_rows, 0
    )
    return (own_map, root_rows)


GROUP = 16


def sweep_kernel(count, size, x_ref, o_ref):
    group = min(count, GROUP)
    span = min(size, 16)
    sub = lax.broadcasted_iota(jnp.int32, (1, size, size), 1)
    lane = lax.broadcasted_iota(jnp.int32, (1, 1, size), 2)

    def one(start):
        o_ref[pl.ds(start, group)] = x_ref[pl.ds(start, group)]
        pl.loop(0, size // span)(lambda turn: part(start))

    def part(start):
        a = o_ref[pl.ds(start, group)]
        for k in range(0, span, 2):
            row0, row1 = a[:, k : k + 1, :], a[:, k + 1 : k + 2, :]
            col0, col1 = a[:, :, k : k + 1], a[:, :, k + 1 : k + 2]
            p, q, r = row0[:, :, k : k + 1], row0[:, :, k + 1 : k + 2], row1[:, :, k + 1 : k + 2]
            inv = 1.0 / (p * r - q * q)
            is0, is1 = lane == k, lane == k + 1
            row0 = jnp.where(is0, 1.0, jnp.where(is1, 0.0, row0))
            row1 = jnp.where(is0, 0.0, jnp.where(is1, 1.0, row1))
            s0 = (r * row0 - q * row1) * inv
            s1 = (p * row1 - q * row0) * inv
            rest = jnp.where(is0 | is1, 0.0, a) - col0 * s0 - col1 * s1
            a = jnp.where(sub == k, s0, jnp.where(sub == k + 1, s1, rest))
        a = jnp.concatenate([a[:, span:], a[:, :span]], axis=1)
        a = jnp.concatenate([a[:, :, span:], a[:, :, :span]], axis=2)
        o_ref[pl.ds(start, group)] = a

    if count == group:
        one(0)
    else:
        pl.loop(0, count // group)(lambda g: one(g * group))


def inverses(blocks):
    count, size, _ = blocks.shape
    return pl.pallas_call(
        functools.partial(sweep_kernel, count, size),
        out_shape=jax.ShapeDtypeStruct(blocks.shape, jnp.float32),
        in_specs=[pl.BlockSpec(memory_space=pltpu.VMEM)],
        out_specs=pl.BlockSpec(memory_space=pltpu.VMEM),
    )(blocks)


def piece_kernel(size, rows, vec_ref, cols_ref, o_ref, coef):
    levels = size.bit_length() - 1
    i = pl.program_id(0)

    def back(x, s):
        return pltpu.roll(x, s, 1)

    def fore(x, s):
        return pltpu.roll(x, size - s, 1)

    @pl.when(i == 0)
    def _():
        def wide(k):
            return jnp.broadcast_to(vec_ref[k : k + 1, :], (8, size))

        a0, a1, al0, al1 = wide(0), wide(1), wide(2), wide(3)
        sh1 = back(al1, 1)
        diag = a0 + a1 + al1 + sh1
        inv = 1.0 / diag
        coef[0] = inv
        lo = -sh1 * inv
        hi = -al1 * inv
        for level in range(levels - 1):
            s = 1 << level
            fix = 1.0 / (1.0 - lo * back(hi, s) - hi * fore(lo, s))
            coef[3 * level + 1] = -lo
            coef[3 * level + 2] = -hi
            coef[3 * level + 3] = fix
            lo, hi = -lo * back(lo, s) * fix, -hi * fore(hi, s) * fix
        g = lo + hi
        h = back(g, size // 2)
        coef[3 * levels - 2] = -g
        coef[3 * levels - 1] = 1.0 / (1.0 - g * h)

    def co(k):
        return coef[k, 0:1, :]

    row = lax.broadcasted_iota(jnp.int32, (rows, size), 0) + i * rows
    col = lax.broadcasted_iota(jnp.int32, (rows, size), 1)
    x = jnp.where(row == col, co(0), 0.0)
    for level in range(levels - 1):
        s = 1 << level
        x = (x + co(3 * level + 1) * back(x, s) + co(3 * level + 2) * fore(x, s)) * co(3 * level + 3)
    x = (x + co(3 * levels - 2) * back(x, size // 2)) * co(3 * levels - 1)
    a0, a1, al0 = vec_ref[0:1, :], vec_ref[1:2, :], vec_ref[2:3, :]
    sh0 = jnp.broadcast_to(vec_ref[4:5, :], (1, size))
    r0, r1 = cols_ref[:, 0:1], cols_ref[:, 1:2]
    vert = jnp.where(row == col, al0 + sh0 + a0, 0.0)
    vert = vert - jnp.where(row == jnp.where(col == size - 1, 0, col + 1), al0, 0.0)
    vert = vert - jnp.where(col == jnp.where(row == size - 1, 0, row + 1), sh0, 0.0)
    x0, x1 = x * a0, x * a1
    o_ref[0, :, :size] = vert - r0 * x0
    o_ref[0, :, size:] = -(r0 * x1)
    o_ref[1, :, :size] = -(r1 * x0)
    o_ref[1, :, size:] = jnp.where(row == col, a1, 0.0) - r1 * x1


def piece_map(across, along):
    size = across.shape[1]
    rows = 32
    vecs = jnp.concatenate([across, along, jnp.roll(along, 1, axis=1), along], axis=0)
    out = pl.pallas_call(
        functools.partial(piece_kernel, size, rows),
        grid=(size // rows,),
        out_shape=jax.ShapeDtypeStruct((2, size, 2 * size), jnp.float32),
        in_specs=[
            pl.BlockSpec((8, size), lambda i: (0, 0)),
            pl.BlockSpec((rows, 2), lambda i: (i, 0)),
        ],
        out_specs=pl.BlockSpec((2, rows, 2 * size), lambda i: (0, i, 0)),
        scratch_shapes=[pltpu.VMEM((3 * (size.bit_length() - 1), 8, size), jnp.float32)],
    )(vecs, across.T)
    return out.reshape(2 * size, 2 * size)


def gather_kernel(slabs, cols, x_ref, o_ref, send, recv, pass_send, pass_recv, own):
    half = cols // 2
    pairs = slabs * half
    slab, col = lax.axis_index("slab"), lax.axis_index("col")
    pair, odd = slab * half + col // 2, lax.rem(col, 2)
    me = slab * cols + col

    def place(q, side):
        return {"slab": q // half, "col": lax.rem(q, half) * 2 + side}

    def index(q, side):
        return q * 2 + side

    def to(step):
        return lax.rem(pair + step, pairs)

    def copy(src, at, sems, step, device):
        return pltpu.make_async_remote_copy(
            src_ref=src,
            dst_ref=o_ref.at[at],
            send_sem=sems[0].at[step],
            recv_sem=sems[1].at[step],
            device_id=device,
            device_id_type=pl.DeviceIdType.MESH,
        )

    barrier = pltpu.get_barrier_semaphore()
    sibling = place(pair, 1 - odd)
    for step in range(1, pairs):
        pl.semaphore_signal(
            barrier, inc=1, device_id=place(to(step), odd), device_id_type=pl.DeviceIdType.MESH
        )
    pl.semaphore_signal(barrier, inc=1, device_id=sibling, device_id_type=pl.DeviceIdType.MESH)
    pl.semaphore_wait(barrier, pairs)

    local_copy = pltpu.make_async_copy(x_ref, o_ref.at[me], own)
    local_copy.start()
    out = [copy(x_ref, me, (send, recv), step, place(to(step), odd)) for step in range(1, pairs)]
    for c in out:
        c.start()
    passed = [copy(x_ref, me, (pass_send, pass_recv), 0, sibling)]
    passed[0].start()
    for step in range(1, pairs):
        at = index(to(pairs - step), odd)
        copy(x_ref, at, (send, recv), step, sibling).wait_recv()
        c = copy(o_ref.at[at], at, (pass_send, pass_recv), step, sibling)
        c.start()
        passed.append(c)
    for step in range(pairs):
        at = index(to(pairs - step), 1 - odd)
        copy(x_ref, at, (pass_send, pass_recv), step, sibling).wait_recv()
    for c in out + passed:
        c.wait_send()
    local_copy.wait()


def gathered(block, number):
    slabs, cols = lax.axis_size("slab"), lax.axis_size("col")
    if cols % 2:
        return lax.all_gather(block, AXES, axis=0)
    pairs = slabs * cols // 2
    return pl.pallas_call(
        functools.partial(gather_kernel, slabs, cols),
        out_shape=jax.ShapeDtypeStruct((slabs * cols,) + block.shape, block.dtype),
        in_specs=[pl.BlockSpec(memory_space=pltpu.VMEM)],
        out_specs=pl.BlockSpec(memory_space=pltpu.VMEM),
        scratch_shapes=[pltpu.SemaphoreType.DMA((pairs,))] * 4 + [pltpu.SemaphoreType.DMA],
        compiler_params=pltpu.CompilerParams(collective_id=number, has_side_effects=True),
    )(block)


def bmm(a, b):
    return jnp.einsum("bij,bjk->bik", a, b, precision=PRODUCT)


def bmm_t(a, b):
    return jnp.einsum("bji,bjk->bik", a, b, precision=PRODUCT)


def t(a):
    return jnp.swapaxes(a, 1, 2)


def row_elements(across, along_prev, along):
    rows, cols = across.shape
    spot = lax.broadcasted_iota(jnp.int32, (rows, cols), 1)
    inner = spot > 0
    diag = jnp.where(inner, jnp.roll(across, 1, axis=1) + across + along_prev + along, 1.0)
    off = jnp.where(inner, across, 0.0)
    i = lax.broadcasted_iota(jnp.int32, (1, cols, cols), 1)
    j = lax.broadcasted_iota(jnp.int32, (1, cols, cols), 2)
    bb = jnp.where(i == j, diag[:, :, None], 0.0)
    bb = bb - jnp.where(j == i + 1, off[:, :, None], 0.0) - jnp.where(i == j + 1, off[:, None, :], 0.0)
    tb = jnp.where(i == j, -jnp.where(inner, along_prev, 0.0)[:, :, None], 0.0)
    tt = jnp.zeros_like(bb)
    first = jnp.where(spot == 1, -across[:, :1], 0.0)
    last = jnp.where(spot == cols - 1, -across[:, cols - 1 :], 0.0)
    fb = jnp.stack([first, last], axis=2)
    return tt, tb, bb, jnp.zeros_like(fb), fb, jnp.zeros((rows, 2, 2), jnp.float32)


def merge_elements(parts):
    (tta, ttb), (tba, tbb), (bba, bbb), (fta, ftb), (fba, fbb), (kka, kkb) = [
        (p[0::2], p[1::2]) for p in parts
    ]
    n, k = tta.shape[1], fta.shape[2]
    w = jnp.concatenate([t(tba), tbb, fba, ftb], axis=2)
    z = bmm(inverses(bba + ttb), w)
    u = bmm_t(w, z)
    zero = jnp.zeros_like(fta)
    zk = jnp.zeros_like(kka)
    kk = jnp.concatenate(
        [jnp.concatenate([kka, zk], axis=2), jnp.concatenate([zk, kkb], axis=2)], axis=1
    )
    return (
        tta - u[:, :n, :n],
        -u[:, :n, n : 2 * n],
        bbb - u[:, n : 2 * n, n : 2 * n],
        jnp.concatenate([fta, zero], axis=2) - u[:, :n, 2 * n :],
        jnp.concatenate([zero, fbb], axis=2) - u[:, n : 2 * n, 2 * n :],
        kk - u[:, 2 * n :, 2 * n :],
    )


def ring_solve(d, link, rhs):
    count, n = d.shape[0], d.shape[1]
    if count == 1:
        return bmm(inverses(d + link + t(link)), rhs)
    w = jnp.concatenate([t(link[0::2]), link[1::2], rhs[0::2]], axis=2)
    z = bmm(inverses(d[0::2]), w)
    u = bmm_t(w[:, :, : 2 * n], z)
    after = jnp.roll(u, -1, axis=0)
    d_next = d[1::2] - u[:, n:, n : 2 * n] - after[:, :n, :n]
    r_next = rhs[1::2] - u[:, n:, 2 * n :] - after[:, :n, 2 * n :]
    odd = ring_solve(d_next, -u[:, :n, n : 2 * n], r_next)
    both = jnp.concatenate([jnp.roll(odd, 1, axis=0), odd], axis=1)
    even = z[:, :, 2 * n :] - bmm(z[:, :, : 2 * n], both)
    return jnp.stack([even, odd], axis=1).reshape(rhs.shape)


def local_rows(classes, across_coeff, along_coeff):
    own_across = lookup(classes, across_coeff)
    own_along = lookup(classes, along_coeff)
    devices = lax.axis_size(AXES)
    me = lax.axis_index(AXES)
    size = classes.shape[1]
    cols = classes.shape[0] * devices
    height = size // devices
    everyone = gathered(classes, 0).reshape(cols, size)
    own_map = piece_map(own_across, own_along)
    padded = jnp.concatenate([everyone[:, size - 1 :], everyone], axis=1)
    mine = lax.dynamic_slice_in_dim(padded, me * height, height + 1, 1)
    across = lookup(mine, across_coeff).T
    along = lookup(mine, along_coeff).T
    parts = row_elements(across[1:], along[:-1], along[1:])
    while parts[0].shape[0] > 1:
        parts = merge_elements(parts)
    tt, tb, bb, ft, fb, kk = [p[0] for p in parts]

    def sides(f):
        return f.reshape(f.shape[0], height, 2).swapaxes(1, 2).reshape(f.shape[0], 2 * height)

    ft, fb = sides(ft), sides(fb)
    kk = sides(sides(kk).T)
    wide = jnp.concatenate(
        [jnp.concatenate([tt, tb], axis=1), jnp.concatenate([bb, ft, fb], axis=1)], axis=0
    )
    lanes = wide.shape[1]
    kk_rows = kk.size // lanes
    wide = jnp.concatenate([wide, kk.reshape(kk_rows, lanes)], axis=0)
    wide = gathered(wide, 1)
    top, low = wide[:, :cols], wide[:, cols : 2 * cols]
    k = 2 * height
    tt, tb = top[:, :, :cols], top[:, :, cols:]
    bb, ft, fb = low[:, :, :cols], low[:, :, cols : cols + k], low[:, :, cols + k :]
    kk = wide[:, 2 * cols :].reshape(devices, k, k)
    share = 2 * size // devices
    start = me * share
    side = start // size
    r0 = start - side * size
    s0 = r0 // height
    strip = lax.broadcasted_iota(jnp.int32, (devices, 1, 1), 0)

    def cut(f, a):
        return lax.dynamic_slice(f, (s0 + a, 0, side * height), (1, f.shape[1], height))[0]

    def at(f, a):
        return jnp.where(strip == s0 + a, f[None], 0.0)

    def rhs_of(f):
        return jnp.concatenate([at(cut(f, 0), 0), at(cut(f, 1), 1)], axis=2)

    rhs = rhs_of(fb) + jnp.roll(rhs_of(ft), -1, axis=0)
    x = ring_solve(bb + jnp.roll(tt, -1, axis=0), tb, rhs)
    x = jnp.concatenate([jnp.roll(x, 1, axis=0), x], axis=1)
    f = jnp.concatenate([ft, fb], axis=1)
    k_rows = jnp.concatenate([at(cut(kk, 0).T, 0), at(cut(kk, 1).T, 1)], axis=1)
    rows = k_rows - bmm_t(x, f)
    rows = rows.reshape(devices, share, 2, height).transpose(1, 2, 0, 3).reshape(share, 2 * size)

    first_ac = lookup(everyone[:1], across_coeff)
    last_ac = lookup(everyone[cols - 1 :], across_coeff)
    al = lookup(everyone[:1], along_coeff)
    sh = jnp.roll(al, 1, axis=1)
    zero = jnp.zeros_like(al)
    on = jnp.concatenate([first_ac + al + sh, last_ac], axis=1)
    below = jnp.concatenate([al, zero], axis=1)
    above = jnp.concatenate([sh, zero], axis=1)
    row = lax.broadcasted_iota(jnp.int32, (share, 2 * size), 0) + start
    col = lax.broadcasted_iota(jnp.int32, (share, 2 * size), 1)
    rows = rows + jnp.where(row == col, on, 0.0)
    rows = rows - jnp.where((row == (col + 1) % size) & (row < size) & (col < size), below, 0.0)
    rows = rows - jnp.where((col == (row + 1) % size) & (row < size) & (col < size), above, 0.0)
    return own_map, rows


def local(classes, across_coeff, along_coeff):
    devices = lax.axis_size(AXES)
    cols = classes.shape[0] * devices
    if 4 * cols <= classes.shape[1] and 4 * classes.shape[1] == cols * devices:
        return local_rows(classes, across_coeff, along_coeff)
    return local_columns(classes, across_coeff, along_coeff)


def solution(mesh):
    placed = (P(("slab", "col"), None), P(), P())
    return jax.shard_map(
        local,
        mesh=mesh,
        in_specs=placed,
        out_specs=(P(("slab", "col"), None), P(("slab", "col"), None)),
        check_vma=False,
    )
```
